32 devices in a mesh: sector: 8 (over z, y), term: 4 (over x, core).
Axes of the slice: x: 2, y: 2, z: 4, core: 2. Of those that a mesh axis runs over, the one named last changes fastest.
Arguments:
- trial_vector: bfloat16 [8, 512, 512], P('sector'), may hold values from -6 to 6
- sector_energy: float32 [8], P('sector'), may hold values from 0.5 to 4
- left_blocks: bfloat16 [64, 8, 512, 512], P('term', 'sector'), may hold values from -0.25 to 0.25
- right_blocks: bfloat16 [64, 8, 512, 512], P('term', 'sector'), may hold values from -0.046875 to 0.046875
- source_sector: int32 [64, 8], P('term', 'sector'), may hold values from 0 to 7
- coupled: int32 [64, 8], P('term', 'sector'), may hold values from 0 to 1, as said below
Outputs:
- applied: float32 [8, 512, 512], P('sector', 'term')
- ritz_values: float32 [2], replicated
The draws below stay inside these ranges and needn't reach their ends.
Inputs may be any that keep to these rules, and one draw needn't show every extreme that they name: Each target sector has its own density of coupled terms.
All inputs are finite; a program needn't handle non-finite values.
Results may differ from the reference program's by a relative error of at most 0.004.
Values may be sent and summed in bfloat16 or wider, within the bound.
A program may use at most 64 MiB of HBM per device.

```python
import math
import jax
import jax.numpy as jnp
from jax import lax

B = 512
SECT = 8
TERMS = 64


def draw_coupled(key, part):
    level_key = jax.random.fold_in(key, 11)
    pick_key = jax.random.fold_in(key, 23)
    levels = jax.random.randint(level_key, (SECT,), 1, 5)
    picks = jax.random.randint(pick_key, (TERMS, SECT), 0, 4)
    return (picks < levels[None, :]).astype(jnp.int32)


def set_ends(entries, rng, low, largest):
    dims = entries.shape
    index_at = [jax.random.randint(jax.random.fold_in(rng, axis), (), 0, dims[axis]) for axis in range(len(dims))]
    entries = entries.at[tuple(index_at)].set(low)
    longest = dims.index(max(dims))
    index_at[longest] = (index_at[longest] + 1) % dims[longest]
    return entries.at[tuple(index_at)].set(largest)


def steps_of(rng, dims, cuts, low, largest):
    factor_of = 1.0
    for dim, parts in cuts:
        steps = jax.random.uniform(jax.random.fold_in(jax.random.fold_in(rng, 6), dim), (parts,), jnp.float32, low / len(cuts), largest / len(cuts))
        factor_of = factor_of * jnp.repeat(jnp.exp(steps), dims[dim] // parts).reshape((-1,) + (1,) * (len(dims) - 1 - dim))
    return factor_of


def centred(own_key, extent, width, bound, pieces=(), held_as=jnp.bfloat16):
    factor_of = steps_of(own_key, extent, pieces, -0.22, 0.18) if pieces else 1.0
    drawn = jax.random.normal(own_key, extent, jnp.float32) * width * factor_of
    return jnp.minimum(jnp.maximum(drawn, -bound), bound).astype(held_as)


def setup_inputs(seed: int = 0) -> dict:
    key_of = jax.random.split(jax.random.key(seed), 7)
    trial_vector = centred(key_of[0], (SECT, B, B), 1.0, 6.0, ((0, 8),))
    sector_energy = jnp.clip(jnp.exp(math.log(4.0) - 2.0794415 * jax.random.uniform(key_of[1], (SECT,), jnp.float32) ** steps_of(key_of[1], (SECT,), ((0, 8),), -0.2, 0.2)), 0.5, 4.0)
    left_blocks = centred(key_of[2], (TERMS, SECT, B, B), B ** -0.5, 0.25, ((0, 4), (1, 8)))
    right_blocks = centred(key_of[3], (TERMS, SECT, B, B), (B * TERMS // 2) ** -0.5, 0.046875, ((0, 4), (1, 8)))
    source_sector = set_ends(jax.random.randint(key_of[4], (TERMS, SECT), 0, SECT), jax.random.fold_in(key_of[4], 1), 0, SECT - 1).astype(jnp.int32)
    coupled = draw_coupled(jax.random.fold_in(key_of[6], 71), 0)
    return {"trial_vector": trial_vector, "sector_energy": sector_energy, "left_blocks": left_blocks, "right_blocks": right_blocks, "source_sector": source_sector, "coupled": coupled}


def apply_all(vector, sector_energy, left_blocks, right_blocks, source_sector, coupled):

    def sector_fn(sector_idx):

        def term_step(total, term_idx):

            def compute(carry):
                block = vector[source_sector[term_idx, sector_idx]]
                middle = jnp.dot(left_blocks[term_idx, sector_idx], block, preferred_element_type=jnp.float32).astype(jnp.bfloat16)
                return carry + jnp.dot(middle, right_blocks[term_idx, sector_idx], preferred_element_type=jnp.float32)
            return (lax.cond(coupled[term_idx, sector_idx] > 0, compute, lambda carry: carry, total), None)
        start = jnp.zeros((B, B), jnp.float32)
        total, _ = lax.scan(term_step, start, jnp.arange(TERMS, dtype=jnp.int32))
        return total + sector_energy[sector_idx] * vector[sector_idx].astype(jnp.float32)
    return lax.map(sector_fn, jnp.arange(SECT, dtype=jnp.int32))

def reference(trial_vector, sector_energy, left_blocks, right_blocks, source_sector, coupled):
    first = apply_all(trial_vector, sector_energy, left_blocks, right_blocks, source_sector, coupled)
    trial = trial_vector.astype(jnp.float32)
    rayleigh = jnp.sum(trial * first) / jnp.sum(trial * trial)
    residual = first - rayleigh * trial
    vector_rms = jnp.sqrt(jnp.mean(residual * residual) + 1e-06)
    next_vector = (residual / vector_rms).astype(jnp.bfloat16)
    applied = apply_all(next_vector, sector_energy, left_blocks, right_blocks, source_sector, coupled)
    return (applied, jnp.stack([rayleigh, vector_rms]))
```

```python
import functools
import jax
import jax.numpy as jnp
from jax import lax
from jax.experimental import pallas as pl
from jax.experimental.pallas import tpu as pltpu
from jax.sharding import PartitionSpec as P

MESH = pl.DeviceIdType.MESH
F32 = jnp.float32
BF16 = jnp.bfloat16
CORES = 2
CHUNKS = 2


def plan(sectors, terms, order):
    na = 4 if sectors % 4 == 0 else sectors
    nb = sectors // na
    nx = terms // CORES
    share = order // terms
    early = 48 if (nx == 2 and share == 128) else 0
    return na, nb, nx, share, early


def kernel(
    sectors, terms, count, order,
    trial_ref, energy_ref, left_hbm, right_hbm, source_ref, coupled_ref,
    out_ref, ritz_ref,
    left, right, vecs, mid, acc, rs_core, rs_send, rs_x, red_term, red_sector, red_send, own,
    send_sem, recv_sem, left_sem, right_sem,
):
    na, nb, nx, share, early = plan(sectors, terms, order)
    width = order // CHUNKS
    s = lax.axis_index("sector")
    t = lax.axis_index("term")
    a, b = s // nb, lax.rem(s, nb)
    x, core = t // CORES, lax.rem(t, CORES)
    other = 1 - core

    def vec(g, c):
        return vecs[g * CHUNKS + c]

    ids = {}
    pending = []

    def sem_id(key):
        return ids.setdefault(key, len(ids))

    def send(src, dst, key, device):
        k = sem_id(key)
        copy = pltpu.make_async_remote_copy(
            src_ref=src, dst_ref=dst, send_sem=send_sem.at[k], recv_sem=recv_sem.at[k],
            device_id=device, device_id_type=MESH,
        )
        copy.start()
        pending.append(copy)

    def recv(dst, key):
        k = sem_id(key)
        pltpu.make_async_remote_copy(
            src_ref=dst, dst_ref=dst, send_sem=send_sem.at[k], recv_sem=recv_sem.at[k],
            device_id=(s, t), device_id_type=MESH,
        ).wait_recv()

    def flush():
        for copy in pending:
            copy.wait_send()
        pending.clear()

    def at_a(i):
        return (lax.rem(a + i, na) * nb + b, t)

    def at_b(j):
        return (a * nb + lax.rem(b + j, nb), t)

    def at_x(k):
        return (s, lax.rem(x + k, nx) * CORES + core)

    at_core = (s, x * CORES + other)

    def sec(i, j):
        return lax.rem(a - i + na, na) * nb + lax.rem(b - j + nb, nb)

    def quarter(k, c):
        return lax.rem(x - k + nx, nx) * CORES + c

    def rows(part, low=0, size=None):
        size = share - low if size is None else size
        return pl.ds(pl.multiple_of(part * share + low, 16), size)

    for k in range(count):
        pltpu.make_async_copy(left_hbm.at[k, 0], left.at[k], left_sem.at[k]).start()
    for k in range(count):
        pltpu.make_async_copy(right_hbm.at[k, 0], right.at[k], right_sem.at[k]).start()

    barrier = pltpu.get_barrier_semaphore()
    for k in range(1, terms):
        pl.semaphore_signal(barrier, inc=1, device_id=(s, lax.rem(t + k, terms)), device_id_type=MESH)
    for k in range(1, sectors):
        pl.semaphore_signal(barrier, inc=1, device_id=(lax.rem(s + k, sectors), t), device_id_type=MESH)
    for c in range(CHUNKS):
        vec(0, c)[s] = trial_ref[0, :, c * width:(c + 1) * width]
    pl.semaphore_wait(barrier, terms + sectors - 2)

    def gather(g, c):
        def ref(sector, where):
            return vec(g, c).at[sector, where]

        def push(sector, where, key, device):
            send(ref(sector, where), ref(sector, where), (g, c) + key, device)

        def pull(sector, where, key):
            recv(ref(sector, where), (g, c) + key)

        mine = rows(t)
        peer_early = rows(quarter(1, core), 0, early) if early else None

        def first():
            if g == 1:
                for k in range(1, nx):
                    push(s, mine, ("x0", k), at_x(k))
                push(s, mine, ("c", 0, 0, 0), at_core)
            for i in range(na - 1, 0, -1):
                push(s, mine, ("a", i), at_a(i))

        def second():
            if g == 1:
                for k in range(1, nx):
                    pull(s, rows(quarter(k, core)), ("x0", k))
            if early:
                for i in range(na - 1, 0, -1):
                    push(s, peer_early, ("aq", i), at_a(i))
            if g == 1:
                for k in range(1, nx):
                    push(s, rows(quarter(k, core)), ("c", 0, 0, k), at_core)

        def distribute(i, j):
            for k in range(1, nx):
                push(sec(i, j), rows(t, early), ("x", i, j, k), at_x(k))
            push(sec(i, j), mine, ("c", i, j, 0), at_core)

        def third():
            for i in range(na):
                if i:
                    pull(sec(i, 0), mine, ("a", i))
                    if early:
                        pull(sec(i, 0), peer_early, ("aq", i))
                for j in range(1, nb):
                    push(sec(i, 0), mine, ("b", i, j), at_b(j))
                    if early:
                        push(sec(i, 0), peer_early, ("bq", i, j), at_b(j))
                if i:
                    distribute(i, 0)

        def fourth():
            for i in range(na):
                for j in range(1, nb):
                    pull(sec(i, j), mine, ("b", i, j))
                    if early:
                        pull(sec(i, j), peer_early, ("bq", i, j))
                    distribute(i, j)

        order_of = [(i, 0) for i in range(1, na)] + [(i, j) for i in range(na) for j in range(1, nb)]

        def fifth():
            for i, j in order_of:
                for k in range(1, nx):
                    pull(sec(i, j), rows(quarter(k, core), early), ("x", i, j, k))
                    push(sec(i, j), rows(quarter(k, core)), ("c", i, j, k), at_core)

        def last():
            for i, j in ([(0, 0)] if g == 1 else []) + order_of:
                for k in range(nx):
                    pull(sec(i, j), rows(quarter(k, other)), ("c", i, j, k))

        return [first, second, third, fourth, fifth, last]

    def middles(g, c, low, high):
        def step(k, carry):
            made = jnp.dot(left[k], vec(g, c)[source_ref[k, 0]], preferred_element_type=F32)
            mid[k, :, c * width:(c + 1) * width] = jnp.where(coupled_ref[k, 0] > 0, made, 0.0).astype(BF16)
            return carry

        lax.fori_loop(low, high, step, 0)

    def products(c, low, high):
        cols = slice(c * width, (c + 1) * width)
        if low == 0:
            acc[c] = jnp.dot(mid[0], right[0, :, cols], preferred_element_type=F32)
            low = 1

        def step(k, carry):
            acc[c] += jnp.dot(mid[k], right[k, :, cols], preferred_element_type=F32)
            return carry

        lax.fori_loop(low, high, step, 0)

    def reduce_core(g, c):
        for k in range(nx):
            part = lax.rem(x + k, nx) * CORES + other
            send(acc.at[c, rows(part)], rs_core.at[c, k], ("rc", g, c, k), at_core)

    def reduce_x(g, c):
        for k in range(1, nx):
            recv(rs_core.at[c, k], ("rc", g, c, k))
            part = lax.rem(x + k, nx) * CORES + core
            rs_send[c, k - 1] = acc[c, rows(part)] + rs_core[c, k]
            send(rs_send.at[c, k - 1], rs_x.at[c, k - 1], ("rx", g, c, k), at_x(k))

    def reduce_last(g, c):
        recv(rs_core.at[c, 0], ("rc", g, c, 0))
        total = acc[c, rows(t)] + rs_core[c, 0]
        for k in range(1, nx):
            recv(rs_x.at[c, k - 1], ("rx", g, c, k))
            total = total + rs_x[c, k - 1]
        return total

    def sum_term(n, tile):
        red_send[n, 0] = tile
        red_term[n, t] = tile
        for k in range(1, terms):
            send(red_send.at[n, 0], red_term.at[n, t], ("st", n, k), (s, lax.rem(t + k, terms)))

    def sum_sector(n):
        for k in range(1, terms):
            recv(red_term.at[n, lax.rem(t - k + terms, terms)], ("st", n, k))
        tile = red_term[n, 0]
        for k in range(1, terms):
            tile = tile + red_term[n, k]
        red_send[n, 1] = tile
        red_sector[n, s] = tile
        for k in range(1, sectors):
            send(red_send.at[n, 1], red_sector.at[n, s], ("ss", n, k), (lax.rem(s + k, sectors), t))

    def sum_last(n):
        for k in range(1, sectors):
            recv(red_sector.at[n, lax.rem(s - k + sectors, sectors)], ("ss", n, k))
        tile = red_sector[n, 0]
        for k in range(1, sectors):
            tile = tile + red_sector[n, k]
        return tile

    energy = energy_ref[0]
    half = count // 2

    def application(g, between):
        steps = [gather(g, c) for c in range(CHUNKS)]
        for c in range(CHUNKS):
            steps[c][0]()
        for c in range(CHUNKS):
            steps[c][1]()
        for stage in range(2, 6):
            steps[0][stage]()
        marks = [0, count // 4, half, 3 * count // 4, count]
        for n in range(4):
            if g == 0:
                for k in range(marks[n], marks[n + 1]):
                    pltpu.make_async_copy(left_hbm.at[k, 0], left.at[k], left_sem.at[k]).wait()
            middles(g, 0, marks[n], marks[n + 1])
            steps[1][2 + n]()
        middles(g, 1, 0, count)
        if g == 0:
            for k in range(count):
                pltpu.make_async_copy(right_hbm.at[k, 0], right.at[k], right_sem.at[k]).wait()
        products(0, 0, count)
        reduce_core(g, 0)
        products(1, 0, half)
        reduce_x(g, 0)
        products(1, half, count)
        reduce_core(g, 1)
        between()
        reduce_x(g, 1)

    def trial_rows(c):
        return trial_ref[0, rows(t), c * width:(c + 1) * width].astype(F32)

    sub = lax.broadcasted_iota(jnp.int32, (8, 128), 0)

    def start_rayleigh():
        cross = F32(0.0)
        square = F32(0.0)
        for c in range(CHUNKS):
            cross += jnp.sum(acc[c] * trial_ref[0, :, c * width:(c + 1) * width].astype(F32))
            square += jnp.sum(trial_rows(c) * trial_rows(c))
        sum_term(0, jnp.where(sub == 0, cross + energy * square, square))

    application(0, start_rayleigh)
    sum_sector(0)
    for c in range(CHUNKS):
        own[c] = reduce_last(0, c) + energy * trial_rows(c)
    sums = sum_last(0)
    rayleigh = sums[0, 0] / sums[1, 0]
    total = F32(0.0)
    for c in range(CHUNKS):
        residual = own[c] - rayleigh * trial_rows(c)
        own[c] = residual
        total += jnp.sum(residual * residual)
    sum_term(1, jnp.full((8, 128), total, F32))
    sum_sector(1)
    flush()
    entries = float(sectors * order * order)
    rms_tile = jnp.sqrt(sum_last(1) / entries + 1e-06)
    rms = rms_tile[0, 0]
    ritz_ref[0] = rayleigh
    ritz_ref[1] = rms
    for c in range(CHUNKS):
        vec(1, c)[s, rows(t)] = (own[c] / rms).astype(BF16)
    application(1, lambda: None)
    for c in range(CHUNKS):
        scaled = energy * vec(1, c)[s, rows(t)].astype(F32)
        out_ref[0, :, c * width:(c + 1) * width] = reduce_last(1, c) + scaled
    flush()


def solution(mesh):
    sectors, terms = mesh.shape["sector"], mesh.shape["term"]

    def body(trial_vector, sector_energy, left_blocks, right_blocks, source_sector, coupled):
        count, order = left_blocks.shape[0], left_blocks.shape[2]
        na, nb, nx, share, early = plan(sectors, terms, order)
        width = order // CHUNKS
        sems = 2 * CHUNKS * (nx + 2 * na + 2 * sectors + sectors * nx * 2 + 2 * nx) + 2 * (sectors + terms)
        vmem = pl.BlockSpec(memory_space=pltpu.VMEM)
        smem = pl.BlockSpec(memory_space=pltpu.SMEM)
        hbm = pl.BlockSpec(memory_space=pl.ANY)
        return pl.pallas_call(
            functools.partial(kernel, sectors, terms, count, order),
            out_shape=(
                jax.ShapeDtypeStruct((1, share, order), F32),
                jax.ShapeDtypeStruct((2,), F32),
            ),
            in_specs=[vmem, smem, hbm, hbm, smem, smem],
            out_specs=(vmem, smem),
            scratch_shapes=[
                pltpu.VMEM((count, order, order), BF16),
                pltpu.VMEM((count, order, order), BF16),
                [pltpu.VMEM((sectors, order, width), BF16) for _ in range(2 * CHUNKS)],
                pltpu.VMEM((count, order, order), BF16),
                pltpu.VMEM((CHUNKS, order, width), F32),
                pltpu.VMEM((CHUNKS, nx, share, width), F32),
                pltpu.VMEM((CHUNKS, nx - 1, share, width), F32),
                pltpu.VMEM((CHUNKS, nx - 1, share, width), F32),
                pltpu.VMEM((2, terms, 8, 128), F32),
                pltpu.VMEM((2, sectors, 8, 128), F32),
                pltpu.VMEM((2, 2, 8, 128), F32),
                pltpu.VMEM((CHUNKS, share, width), F32),
                pltpu.SemaphoreType.DMA((sems,)),
                pltpu.SemaphoreType.DMA((sems,)),
                pltpu.SemaphoreType.DMA((count,)),
                pltpu.SemaphoreType.DMA((count,)),
            ],
            compiler_params=pltpu.CompilerParams(
                collective_id=0, has_side_effects=True, vmem_limit_bytes=56 * 1024 * 1024
            ),
        )(trial_vector, sector_energy, left_blocks, right_blocks, source_sector, coupled)

    return jax.shard_map(
        body,
        mesh=mesh,
        in_specs=(
            P("sector", None, None),
            P("sector"),
            P("term", "sector", None, None),
            P("term", "sector", None, None),
            P("term", "sector"),
            P("term", "sector"),
        ),
        out_specs=(P("sector", "term", None), P()),
        check_vma=False,
    )
```

```python
import functools
import jax
import jax.numpy as jnp
from jax import lax
from jax.experimental import pallas as pl
from jax.experimental.pallas import tpu as pltpu
from jax.sharding import PartitionSpec as P

MESH = pl.DeviceIdType.MESH
F32 = jnp.float32
BF16 = jnp.bfloat16
CORES = 2
CHUNKS = 2


def plan(sectors, terms, order):
    na = 4 if sectors % 4 == 0 else sectors
    nb = sectors // na
    nx = terms // CORES
    share = order // terms
    early = 32 if (nx == 2 and share == 128) else 0
    return na, nb, nx, share, early


def kernel(
    sectors, terms, count, order,
    trial_ref, energy_ref, left_hbm, right_hbm, source_ref, coupled_ref,
    out_ref, ritz_ref,
    left, right, vecs, mid, acc, rs_core, rs_send, rs_x, red_term, red_sector, red_send, own,
    send_sem, recv_sem, left_sem, right_sem,
):
    na, nb, nx, share, early = plan(sectors, terms, order)
    width = order // CHUNKS
    s = lax.axis_index("sector")
    t = lax.axis_index("term")
    a, b = s // nb, lax.rem(s, nb)
    x, core = t // CORES, lax.rem(t, CORES)
    other = 1 - core

    def vec(g, c):
        return vecs[g * CHUNKS + c]

    ids = {}
    pending = []

    def sem_id(key):
        return ids.setdefault(key, len(ids))

    def send(src, dst, key, device):
        k = sem_id(key)
        copy = pltpu.make_async_remote_copy(
            src_ref=src, dst_ref=dst, send_sem=send_sem.at[k], recv_sem=recv_sem.at[k],
            device_id=device, device_id_type=MESH,
        )
        copy.start()
        pending.append(copy)

    def recv(dst, key):
        k = sem_id(key)
        pltpu.make_async_remote_copy(
            src_ref=dst, dst_ref=dst, send_sem=send_sem.at[k], recv_sem=recv_sem.at[k],
            device_id=(s, t), device_id_type=MESH,
        ).wait_recv()

    def flush():
        for copy in pending:
            copy.wait_send()
        pending.clear()

    def at_a(i):
        return (lax.rem(a + i, na) * nb + b, t)

    def at_b(j):
        return (a * nb + lax.rem(b + j, nb), t)

    def at_x(k):
        return (s, lax.rem(x + k, nx) * CORES + core)

    at_core = (s, x * CORES + other)

    def sec(i, j):
        return lax.rem(a - i + na, na) * nb + lax.rem(b - j + nb, nb)

    def quarter(k, c):
        return lax.rem(x - k + nx, nx) * CORES + c

    def rows(part, low=0, size=None):
        size = share - low if size is None else size
        return pl.ds(pl.multiple_of(part * share + low, 16), size)

    for k in range(count):
        pltpu.make_async_copy(left_hbm.at[k, 0], left.at[k], left_sem.at[k]).start()
    for k in range(count):
        pltpu.make_async_copy(right_hbm.at[k, 0], right.at[k], right_sem.at[k]).start()

    barrier = pltpu.get_barrier_semaphore()
    for k in range(1, terms):
        pl.semaphore_signal(barrier, inc=1, device_id=(s, lax.rem(t + k, terms)), device_id_type=MESH)
    for k in range(1, sectors):
        pl.semaphore_signal(barrier, inc=1, device_id=(lax.rem(s + k, sectors), t), device_id_type=MESH)
    for c in range(CHUNKS):
        vec(0, c)[s] = trial_ref[0, :, c * width:(c + 1) * width]
    pl.semaphore_wait(barrier, terms + sectors - 2)

    def gather(g, c):
        def ref(sector, where):
            return vec(g, c).at[sector, where]

        def push(sector, where, key, device):
            send(ref(sector, where), ref(sector, where), (g, c) + key, device)

        def pull(sector, where, key):
            recv(ref(sector, where), (g, c) + key)

        mine = rows(t)
        peer_early = rows(quarter(1, core), 0, early) if early else None

        def first():
            if g == 1:
                for k in range(1, nx):
                    push(s, mine, ("x0", k), at_x(k))
                push(s, mine, ("c", 0, 0, 0), at_core)
            for i in range(na - 1, 0, -1):
                push(s, mine, ("a", i), at_a(i))
            for j in range(1, nb):
                push(s, mine, ("b", 0, j), at_b(j))

        def second():
            if g == 1:
                for k in range(1, nx):
                    pull(s, rows(quarter(k, core)), ("x0", k))
            if early:
                for i in range(na - 1, 0, -1):
                    push(s, peer_early, ("aq", i), at_a(i))
                for j in range(1, nb):
                    push(s, peer_early, ("bq", 0, j), at_b(j))
            if g == 1:
                for k in range(1, nx):
                    push(s, rows(quarter(k, core)), ("c", 0, 0, k), at_core)

        def distribute(i, j):
            for k in range(1, nx):
                push(sec(i, j), rows(t, early), ("x", i, j, k), at_x(k))
            push(sec(i, j), mine, ("c", i, j, 0), at_core)

        def third():
            for i in range(1, na):
                pull(sec(i, 0), mine, ("a", i))
                if early:
                    pull(sec(i, 0), peer_early, ("aq", i))
                for j in range(1, nb):
                    push(sec(i, 0), mine, ("b", i, j), at_b(j))
                    if early:
                        push(sec(i, 0), peer_early, ("bq", i, j), at_b(j))
                distribute(i, 0)

        def fourth():
            for i in range(na):
                for j in range(1, nb):
                    pull(sec(i, j), mine, ("b", i, j))
                    if early:
                        pull(sec(i, j), peer_early, ("bq", i, j))
                    distribute(i, j)

        order_of = [(i, 0) for i in range(1, na)] + [(i, j) for i in range(na) for j in range(1, nb)]

        def fifth():
            for i, j in order_of:
                for k in range(1, nx):
                    pull(sec(i, j), rows(quarter(k, core), early), ("x", i, j, k))
                    push(sec(i, j), rows(quarter(k, core)), ("c", i, j, k), at_core)

        def last():
            for i, j in ([(0, 0)] if g == 1 else []) + order_of:
                for k in range(nx):
                    pull(sec(i, j), rows(quarter(k, other)), ("c", i, j, k))

        return [first, second, third, fourth, fifth, last]

    def middles(g, c, low, high):
        def one(k):
            made = jnp.dot(left[k], vec(g, c)[source_ref[k]], preferred_element_type=F32)
            mid[k, :, c * width:(c + 1) * width] = jnp.where(coupled_ref[k] > 0, made, 0.0).astype(BF16)

        def step(n, carry):
            one(low + 2 * n)
            one(low + 2 * n + 1)
            return carry

        lax.fori_loop(0, (high - low) // 2, step, 0)

    def products(c, low, high):
        cols = slice(c * width, (c + 1) * width)
        group = 4

        def part(k):
            total = jnp.dot(mid[k], right[k, :, cols], preferred_element_type=F32)
            for n in range(1, group):
                total += jnp.dot(mid[k + n], right[k + n, :, cols], preferred_element_type=F32)
            return total

        if low == 0:
            acc[c] = part(0)
            low = group

        def step(n, carry):
            acc[c] += part(low + n * group)
            return carry

        lax.fori_loop(0, (high - low) // group, step, 0)

    def reduce_core(g, c):
        for k in range(nx):
            part = lax.rem(x + k, nx) * CORES + other
            send(acc.at[c, rows(part)], rs_core.at[c, k], ("rc", g, c, k), at_core)

    def reduce_x(g, c):
        for k in range(1, nx):
            recv(rs_core.at[c, k], ("rc", g, c, k))
            part = lax.rem(x + k, nx) * CORES + core
            rs_send[c, k - 1] = acc[c, rows(part)] + rs_core[c, k]
            send(rs_send.at[c, k - 1], rs_x.at[c, k - 1], ("rx", g, c, k), at_x(k))

    def reduce_last(g, c):
        recv(rs_core.at[c, 0], ("rc", g, c, 0))
        total = acc[c, rows(t)] + rs_core[c, 0]
        for k in range(1, nx):
            recv(rs_x.at[c, k - 1], ("rx", g, c, k))
            total = total + rs_x[c, k - 1]
        return total

    def sum_term(n, tile):
        red_send[n, 0] = tile
        red_term[n, t] = tile
        for k in range(1, terms):
            send(red_send.at[n, 0], red_term.at[n, t], ("st", n, k), (s, lax.rem(t + k, terms)))

    def sum_sector(n):
        for k in range(1, terms):
            recv(red_term.at[n, lax.rem(t - k + terms, terms)], ("st", n, k))
        tile = red_term[n, 0]
        for k in range(1, terms):
            tile = tile + red_term[n, k]
        red_send[n, 1] = tile
        red_sector[n, s] = tile
        for k in range(1, sectors):
            send(red_send.at[n, 1], red_sector.at[n, s], ("ss", n, k), (lax.rem(s + k, sectors), t))

    def sum_last(n):
        for k in range(1, sectors):
            recv(red_sector.at[n, lax.rem(s - k + sectors, sectors)], ("ss", n, k))
        tile = red_sector[n, 0]
        for k in range(1, sectors):
            tile = tile + red_sector[n, k]
        return tile

    energy = energy_ref[0]
    half = count // 2

    def application(g, between):
        steps = [gather(g, c) for c in range(CHUNKS)]
        steps[0][0]()
        steps[0][1]()
        for c, stage in ((0, 2), (1, 0), (1, 1), (0, 3), (1, 2), (0, 4), (1, 3), (0, 5)):
            steps[c][stage]()
        if g == 0:
            for k in range(count):
                pltpu.make_async_copy(left_hbm.at[k, 0], left.at[k], left_sem.at[k]).wait()
        middles(g, 0, 0, half)
        steps[1][4]()
        middles(g, 0, half, count)
        steps[1][5]()
        middles(g, 1, 0, count)
        if g == 0:
            for k in range(count):
                pltpu.make_async_copy(right_hbm.at[k, 0], right.at[k], right_sem.at[k]).wait()
        products(0, 0, count)
        reduce_core(g, 0)
        products(1, 0, half)
        reduce_x(g, 0)
        products(1, half, count)
        reduce_core(g, 1)
        between()
        reduce_x(g, 1)

    def trial_rows(c):
        return trial_ref[0, rows(t), c * width:(c + 1) * width].astype(F32)

    sub = lax.broadcasted_iota(jnp.int32, (8, 128), 0)

    def start_rayleigh():
        cross = F32(0.0)
        square = F32(0.0)
        for c in range(CHUNKS):
            cross += jnp.sum(acc[c] * trial_ref[0, :, c * width:(c + 1) * width].astype(F32))
            square += jnp.sum(trial_rows(c) * trial_rows(c))
        sum_term(0, jnp.where(sub == 0, cross + energy * square, square))

    application(0, start_rayleigh)
    sum_sector(0)
    for c in range(CHUNKS):
        own[c] = reduce_last(0, c) + energy * trial_rows(c)
    sums = sum_last(0)
    rayleigh = sums[0, 0] / sums[1, 0]
    total = F32(0.0)
    for c in range(CHUNKS):
        residual = own[c] - rayleigh * trial_rows(c)
        own[c] = residual
        total += jnp.sum(residual * residual)
    sum_term(1, jnp.full((8, 128), total, F32))
    sum_sector(1)
    flush()
    entries = float(sectors * order * order)
    rms_tile = jnp.sqrt(sum_last(1) / entries + 1e-06)
    rms = rms_tile[0, 0]
    ritz_ref[0] = rayleigh
    ritz_ref[1] = rms
    for c in range(CHUNKS):
        vec(1, c)[s, rows(t)] = (own[c] / rms).astype(BF16)
    application(1, lambda: None)
    for c in range(CHUNKS):
        scaled = energy * vec(1, c)[s, rows(t)].astype(F32)
        out_ref[0, :, c * width:(c + 1) * width] = reduce_last(1, c) + scaled
    flush()


def solution(mesh):
    sectors, terms = mesh.shape["sector"], mesh.shape["term"]

    def body(trial_vector, sector_energy, left_blocks, right_blocks, source_sector, coupled):
        count, order = left_blocks.shape[0], left_blocks.shape[2]
        na, nb, nx, share, early = plan(sectors, terms, order)
        width = order // CHUNKS
        sems = 2 * CHUNKS * (nx + 2 * na + 2 * sectors + sectors * nx * 2 + 2 * nx) + 2 * (sectors + terms)
        vmem = pl.BlockSpec(memory_space=pltpu.VMEM)
        smem = pl.BlockSpec(memory_space=pltpu.SMEM)
        hbm = pl.BlockSpec(memory_space=pl.ANY)
        return pl.pallas_call(
            functools.partial(kernel, sectors, terms, count, order),
            out_shape=(
                jax.ShapeDtypeStruct((1, share, order), F32),
                jax.ShapeDtypeStruct((2,), F32),
            ),
            in_specs=[vmem, smem, hbm, hbm, smem, smem],
            out_specs=(vmem, smem),
            scratch_shapes=[
                pltpu.VMEM((count, order, order), BF16),
                pltpu.VMEM((count, order, order), BF16),
                [pltpu.VMEM((sectors, order, width), BF16) for _ in range(2 * CHUNKS)],
                pltpu.VMEM((count, order, order), BF16),
                pltpu.VMEM((CHUNKS, order, width), F32),
                pltpu.VMEM((CHUNKS, nx, share, width), F32),
                pltpu.VMEM((CHUNKS, nx - 1, share, width), F32),
                pltpu.VMEM((CHUNKS, nx - 1, share, width), F32),
                pltpu.VMEM((2, terms, 8, 128), F32),
                pltpu.VMEM((2, sectors, 8, 128), F32),
                pltpu.VMEM((2, 2, 8, 128), F32),
                pltpu.VMEM((CHUNKS, share, width), F32),
                pltpu.SemaphoreType.DMA((sems,)),
                pltpu.SemaphoreType.DMA((sems,)),
                pltpu.SemaphoreType.DMA((count,)),
                pltpu.SemaphoreType.DMA((count,)),
            ],
            compiler_params=pltpu.CompilerParams(
                collective_id=0, has_side_effects=True, vmem_limit_bytes=56 * 1024 * 1024
            ),
        )(trial_vector, sector_energy, left_blocks, right_blocks, source_sector.reshape(-1), coupled.reshape(-1))

    return jax.shard_map(
        body,
        mesh=mesh,
        in_specs=(
            P("sector", None, None),
            P("sector"),
            P("term", "sector", None, None),
            P("term", "sector", None, None),
            P("term", "sector"),
            P("term", "sector"),
        ),
        out_specs=(P("sector", "term", None), P()),
        check_vma=False,
    )
```

```python
import functools
import jax
import jax.numpy as jnp
from jax import lax
from jax.experimental import pallas as pl
from jax.experimental.pallas import tpu as pltpu
from jax.sharding import PartitionSpec as P

MESH = pl.DeviceIdType.MESH
F32 = jnp.float32
BF16 = jnp.bfloat16
CORES = 2
CHUNKS = 2


def plan(sectors, terms, order):
    na = 4 if sectors % 4 == 0 else sectors
    nb = sectors // na
    nx = terms // CORES
    share = order // terms
    early = 32 if (nx == 2 and share == 128) else 0
    return na, nb, nx, share, early


def kernel(
    sectors, terms, count, order,
    trial_ref, energy_ref, left_hbm, right_hbm, source_ref, coupled_ref,
    out_ref, ritz_ref,
    left, right, vecs, mid, acc, rs_core, rs_send, rs_x, rs_send2, rs_x2, red_term, red_sector, red_send, own,
    send_sem, recv_sem, left_sem, right_sem,
):
    na, nb, nx, share, early = plan(sectors, terms, order)
    width = order // CHUNKS
    s = lax.axis_index("sector")
    t = lax.axis_index("term")
    a, b = s // nb, lax.rem(s, nb)
    x, core = t // CORES, lax.rem(t, CORES)
    other = 1 - core

    def vec(g, c):
        return vecs[g * CHUNKS + c]

    ids = {}
    pending = []

    def sem_id(key):
        return ids.setdefault(key, len(ids))

    def send(src, dst, key, device):
        k = sem_id(key)
        copy = pltpu.make_async_remote_copy(
            src_ref=src, dst_ref=dst, send_sem=send_sem.at[k], recv_sem=recv_sem.at[k],
            device_id=device, device_id_type=MESH,
        )
        copy.start()
        pending.append(copy)

    def recv(dst, key):
        k = sem_id(key)
        pltpu.make_async_remote_copy(
            src_ref=dst, dst_ref=dst, send_sem=send_sem.at[k], recv_sem=recv_sem.at[k],
            device_id=(s, t), device_id_type=MESH,
        ).wait_recv()

    def flush():
        for copy in pending:
            copy.wait_send()
        pending.clear()

    def at_a(i):
        return (lax.rem(a + i, na) * nb + b, t)

    def at_b(j):
        return (a * nb + lax.rem(b + j, nb), t)

    def at_x(k):
        return (s, lax.rem(x + k, nx) * CORES + core)

    at_core = (s, x * CORES + other)

    def sec(i, j):
        return lax.rem(a - i + na, na) * nb + lax.rem(b - j + nb, nb)

    def quarter(k, c):
        return lax.rem(x - k + nx, nx) * CORES + c

    def rows(part, low=0, size=None):
        size = share - low if size is None else size
        return pl.ds(pl.multiple_of(part * share + low, 16), size)

    for k in range(count):
        pltpu.make_async_copy(left_hbm.at[k, 0], left.at[k], left_sem.at[k]).start()
    for k in range(count):
        pltpu.make_async_copy(right_hbm.at[k, 0], right.at[k], right_sem.at[k]).start()

    barrier = pltpu.get_barrier_semaphore()
    for k in range(1, terms):
        pl.semaphore_signal(barrier, inc=1, device_id=(s, lax.rem(t + k, terms)), device_id_type=MESH)
    for k in range(1, sectors):
        pl.semaphore_signal(barrier, inc=1, device_id=(lax.rem(s + k, sectors), t), device_id_type=MESH)
    for c in range(CHUNKS):
        vec(0, c)[s] = trial_ref[0, :, c * width:(c + 1) * width]
    pl.semaphore_wait(barrier, terms + sectors - 2)

    def gather(g, c):
        def ref(sector, where):
            return vec(g, c).at[sector, where]

        def push(sector, where, key, device):
            send(ref(sector, where), ref(sector, where), (g, c) + key, device)

        def pull(sector, where, key):
            recv(ref(sector, where), (g, c) + key)

        mine = rows(t)
        peer_early = rows(quarter(1, core), 0, early) if early else None

        def first():
            if g == 1:
                for k in range(1, nx):
                    push(s, mine, ("x0", k), at_x(k))
                push(s, mine, ("c", 0, 0, 0), at_core)
            for i in range(na - 1, 0, -1):
                push(s, mine, ("a", i), at_a(i))
            for j in range(1, nb):
                push(s, mine, ("b", 0, j), at_b(j))

        def second():
            if g == 1:
                for k in range(1, nx):
                    pull(s, rows(quarter(k, core)), ("x0", k))
            if early:
                for i in range(na - 1, 0, -1):
                    push(s, peer_early, ("aq", i), at_a(i))
                for j in range(1, nb):
                    push(s, peer_early, ("bq", 0, j), at_b(j))
            if g == 1:
                for k in range(1, nx):
                    push(s, rows(quarter(k, core)), ("c", 0, 0, k), at_core)

        def distribute(i, j):
            for k in range(1, nx):
                push(sec(i, j), rows(t, early), ("x", i, j, k), at_x(k))
            push(sec(i, j), mine, ("c", i, j, 0), at_core)

        def third():
            for i in range(1, na):
                pull(sec(i, 0), mine, ("a", i))
                if early:
                    pull(sec(i, 0), peer_early, ("aq", i))
                for j in range(1, nb):
                    push(sec(i, 0), mine, ("b", i, j), at_b(j))
                    if early:
                        push(sec(i, 0), peer_early, ("bq", i, j), at_b(j))
                distribute(i, 0)

        def fourth():
            for i in range(na):
                for j in range(1, nb):
                    pull(sec(i, j), mine, ("b", i, j))
                    if early:
                        pull(sec(i, j), peer_early, ("bq", i, j))
                    distribute(i, j)

        order_of = [(i, 0) for i in range(1, na)] + [(i, j) for i in range(na) for j in range(1, nb)]

        def fifth():
            for i, j in order_of:
                for k in range(1, nx):
                    pull(sec(i, j), rows(quarter(k, core), early), ("x", i, j, k))
                    push(sec(i, j), rows(quarter(k, core)), ("c", i, j, k), at_core)

        def last():
            for i, j in ([(0, 0)] if g == 1 else []) + order_of:
                for k in range(nx):
                    pull(sec(i, j), rows(quarter(k, other)), ("c", i, j, k))

        return [first, second, third, fourth, fifth, last]

    def middles(g, c, low, high):
        def one(k):
            made = jnp.dot(left[k], vec(g, c)[source_ref[k]], preferred_element_type=F32)
            mid[k, :, c * width:(c + 1) * width] = jnp.where(coupled_ref[k] > 0, made, 0.0).astype(BF16)

        def step(n, carry):
            one(low + 2 * n)
            one(low + 2 * n + 1)
            return carry

        lax.fori_loop(0, (high - low) // 2, step, 0)

    def products(c, low, high):
        cols = slice(c * width, (c + 1) * width)
        group = 4

        def part(k):
            total = jnp.dot(mid[k], right[k, :, cols], preferred_element_type=F32)
            for n in range(1, group):
                total += jnp.dot(mid[k + n], right[k + n, :, cols], preferred_element_type=F32)
            return total

        if low == 0:
            acc[c] = part(0)
            low = group

        def step(n, carry):
            acc[c] += part(low + n * group)
            return carry

        lax.fori_loop(0, (high - low) // group, step, 0)

    def reduce_core(g, c):
        for k in range(nx):
            part = lax.rem(x + k, nx) * CORES + other
            send(acc.at[c, rows(part)], rs_core.at[c, k], ("rc", g, c, k), at_core)

    def reduce_x(g, c):
        for k in range(1, nx):
            recv(rs_core.at[c, k], ("rc", g, c, k))
            part = lax.rem(x + k, nx) * CORES + core
            out, into = (rs_send2, rs_x2) if g else (rs_send, rs_x)
            out[c, k - 1] = (acc[c, rows(part)] + rs_core[c, k]).astype(out.dtype)
            send(out.at[c, k - 1], into.at[c, k - 1], ("rx", g, c, k), at_x(k))

    def reduce_last(g, c):
        recv(rs_core.at[c, 0], ("rc", g, c, 0))
        total = acc[c, rows(t)] + rs_core[c, 0]
        for k in range(1, nx):
            into = rs_x2 if g else rs_x
            recv(into.at[c, k - 1], ("rx", g, c, k))
            total = total + into[c, k - 1].astype(F32)
        return total

    def sum_term(n, tile):
        red_send[n, 0] = tile
        red_term[n, t] = tile
        for k in range(1, terms):
            send(red_send.at[n, 0], red_term.at[n, t], ("st", n, k), (s, lax.rem(t + k, terms)))

    def sum_sector(n):
        for k in range(1, terms):
            recv(red_term.at[n, lax.rem(t - k + terms, terms)], ("st", n, k))
        tile = red_term[n, 0]
        for k in range(1, terms):
            tile = tile + red_term[n, k]
        red_send[n, 1] = tile
        red_sector[n, s] = tile
        for k in range(1, sectors):
            send(red_send.at[n, 1], red_sector.at[n, s], ("ss", n, k), (lax.rem(s + k, sectors), t))

    def sum_last(n):
        for k in range(1, sectors):
            recv(red_sector.at[n, lax.rem(s - k + sectors, sectors)], ("ss", n, k))
        tile = red_sector[n, 0]
        for k in range(1, sectors):
            tile = tile + red_sector[n, k]
        return tile

    energy = energy_ref[0]
    half = count // 2

    def application(g, between):
        steps = [gather(g, c) for c in range(CHUNKS)]
        steps[0][0]()
        steps[0][1]()
        for c, stage in ((0, 2), (1, 0), (1, 1), (0, 3), (1, 2), (0, 4), (1, 3), (0, 5)):
            steps[c][stage]()
        if g == 0:
            for k in range(count):
                pltpu.make_async_copy(left_hbm.at[k, 0], left.at[k], left_sem.at[k]).wait()
        middles(g, 0, 0, half)
        steps[1][4]()
        middles(g, 0, half, count)
        steps[1][5]()
        middles(g, 1, 0, count)
        if g == 0:
            for k in range(count):
                pltpu.make_async_copy(right_hbm.at[k, 0], right.at[k], right_sem.at[k]).wait()
        products(0, 0, count)
        reduce_core(g, 0)
        products(1, 0, half)
        reduce_x(g, 0)
        products(1, half, count)
        reduce_core(g, 1)
        between()
        reduce_x(g, 1)

    def trial_rows(c):
        return trial_ref[0, rows(t), c * width:(c + 1) * width].astype(F32)

    sub = lax.broadcasted_iota(jnp.int32, (8, 128), 0)

    def start_rayleigh():
        cross = F32(0.0)
        square = F32(0.0)
        for c in range(CHUNKS):
            cross += jnp.sum(acc[c] * trial_ref[0, :, c * width:(c + 1) * width].astype(F32))
            square += jnp.sum(trial_rows(c) * trial_rows(c))
        sum_term(0, jnp.where(sub == 0, cross + energy * square, square))

    application(0, start_rayleigh)
    sum_sector(0)
    for c in range(CHUNKS):
        own[c] = reduce_last(0, c) + energy * trial_rows(c)
    sums = sum_last(0)
    rayleigh = sums[0, 0] / sums[1, 0]
    total = F32(0.0)
    for c in range(CHUNKS):
        residual = own[c] - rayleigh * trial_rows(c)
        own[c] = residual
        total += jnp.sum(residual * residual)
    sum_term(1, jnp.full((8, 128), total, F32))
    sum_sector(1)
    flush()
    entries = float(sectors * order * order)
    rms_tile = jnp.sqrt(sum_last(1) / entries + 1e-06)
    rms = rms_tile[0, 0]
    ritz_ref[0] = rayleigh
    ritz_ref[1] = rms
    for c in range(CHUNKS):
        vec(1, c)[s, rows(t)] = (own[c] / rms).astype(BF16)
    application(1, lambda: None)
    for c in range(CHUNKS):
        scaled = energy * vec(1, c)[s, rows(t)].astype(F32)
        out_ref[0, :, c * width:(c + 1) * width] = reduce_last(1, c) + scaled
    flush()


def solution(mesh):
    sectors, terms = mesh.shape["sector"], mesh.shape["term"]

    def body(trial_vector, sector_energy, left_blocks, right_blocks, source_sector, coupled):
        count, order = left_blocks.shape[0], left_blocks.shape[2]
        na, nb, nx, share, early = plan(sectors, terms, order)
        width = order // CHUNKS
        sems = 2 * CHUNKS * (nx + 2 * na + 2 * sectors + sectors * nx * 2 + 2 * nx) + 2 * (sectors + terms)
        vmem = pl.BlockSpec(memory_space=pltpu.VMEM)
        smem = pl.BlockSpec(memory_space=pltpu.SMEM)
        hbm = pl.BlockSpec(memory_space=pl.ANY)
        return pl.pallas_call(
            functools.partial(kernel, sectors, terms, count, order),
            out_shape=(
                jax.ShapeDtypeStruct((1, share, order), F32),
                jax.ShapeDtypeStruct((2,), F32),
            ),
            in_specs=[vmem, smem, hbm, hbm, smem, smem],
            out_specs=(vmem, smem),
            scratch_shapes=[
                pltpu.VMEM((count, order, order), BF16),
                pltpu.VMEM((count, order, order), BF16),
                [pltpu.VMEM((sectors, order, width), BF16) for _ in range(2 * CHUNKS)],
                pltpu.VMEM((count, order, order), BF16),
                pltpu.VMEM((CHUNKS, order, width), F32),
                pltpu.VMEM((CHUNKS, nx, share, width), F32),
                pltpu.VMEM((CHUNKS, nx - 1, share, width), F32),
                pltpu.VMEM((CHUNKS, nx - 1, share, width), F32),
                pltpu.VMEM((CHUNKS, nx - 1, share, width), BF16),
                pltpu.VMEM((CHUNKS, nx - 1, share, width), BF16),
                pltpu.VMEM((2, terms, 8, 128), F32),
                pltpu.VMEM((2, sectors, 8, 128), F32),
                pltpu.VMEM((2, 2, 8, 128), F32),
                pltpu.VMEM((CHUNKS, share, width), F32),
                pltpu.SemaphoreType.DMA((sems,)),
                pltpu.SemaphoreType.DMA((sems,)),
                pltpu.SemaphoreType.DMA((count,)),
                pltpu.SemaphoreType.DMA((count,)),
            ],
            compiler_params=pltpu.CompilerParams(
                collective_id=0, has_side_effects=True, vmem_limit_bytes=56 * 1024 * 1024
            ),
        )(trial_vector, sector_energy, left_blocks, right_blocks, source_sector.reshape(-1), coupled.reshape(-1))

    return jax.shard_map(
        body,
        mesh=mesh,
        in_specs=(
            P("sector", None, None),
            P("sector"),
            P("term", "sector", None, None),
            P("term", "sector", None, None),
            P("term", "sector"),
            P("term", "sector"),
        ),
        out_specs=(P("sector", "term", None), P()),
        check_vma=False,
    )
```
